32 devices in a mesh: groups: 2 (over y), blk: 4 (over z), det: 2 (over x), sub: 2 (over core).
Axes of the slice: x: 2, y: 2, z: 4, core: 2. Of those that a mesh axis runs over, the one named last changes fastest.
Arguments:
- data: bfloat16 [128, 16, 256], P(('groups', 'blk', 'det')), parts along dimension 0, may hold values from -6 to 6
- templates: bfloat16 [32, 16, 256], P(('groups', 'blk')), parts along dimension 0
- bin_cuts: int32 [32, 15], P(('groups', 'blk')), parts along dimension 0, may hold values from 1 to 2047, as said below
- trig_template: int32 [16, 2, 128], P(('groups', 'blk', 'det'), 'sub'), parts along dimension 0, may hold values from 0 to 15
- trig_pair: int32 [16, 2, 128], P(('groups', 'blk', 'det'), 'sub'), parts along dimension 0, may hold values from 0 to 63, as said below
- trig_tile: int32 [16, 2, 128], P(('groups', 'blk', 'det'), 'sub'), parts along dimension 0, may hold values from 0 to 7
Outputs:
- peak_snr: float32 [128, 2048], P(('groups', 'blk', 'det'), 'sub'), parts along dimension 0
- chi_snr: float32 [16, 2, 128, 128], P(('groups', 'blk', 'det'), 'sub'), parts along dimension 0
The draws below stay inside these ranges and needn't reach their ends.
There are 2 independent parts, one for each index of `groups`. The reference program is written for one: setup_inputs(seed, part) draws one part's arguments, and reference() takes and returns one part's arrays. A program takes and returns all parts, laid end to end along the dimension named above; each array names one. Nothing has to cross between parts.
Inputs may be any that keep to these rules, and one draw needn't show every extreme that they name: `trig_pair`: in each list [b, h], at most 32 entries lie in any one group of 8 consecutive data block ids that starts at a multiple of 8; one such group holds exactly 32 entries of every list. `bin_cuts`: each row is strictly increasing.
All inputs are finite; a program needn't handle non-finite values.
Results may differ from the reference program's by a relative error of at most 0.0035.
Values may be sent and summed in bfloat16 or wider, within the bound.
A program may use at most 64 MiB of HBM per device.

```python
import math
import jax
import jax.numpy as jnp
from jax import lax

FMAJ = 16
FMIN = 128
FREQS = 2048
NBINS = 16
TILE_STEPS = 8
TEMPLATES = 16
PAIR_DEV = 8
BLOCKS = 8
PAIRS = 64
HALVES = 2
TILES = 8
TRIG_DEV = 128
PCAP = 32


def draw_templates(key, part):
    shape = (TEMPLATES, FMAJ, 2 * FMIN)
    base = jax.random.normal(jax.random.fold_in(key, 11), shape, jnp.float32)
    column = jnp.exp(jax.random.uniform(jax.random.fold_in(key, 12), (FMAJ, FMIN), jnp.float32, -1.15, 1.15))
    row_scale = jnp.exp(jax.random.uniform(jax.random.fold_in(key, 13), (TEMPLATES, 1, 1), jnp.float32, -1.15, 1.15))
    column = jnp.concatenate([column, column], axis=1)
    return (base * column[None] * row_scale).astype(jnp.bfloat16)


def draw_bin_cuts(key, part):
    keys = jax.random.split(jax.random.fold_in(key, 21), TEMPLATES)

    def one_row(row_key):
        chosen = jax.random.permutation(row_key, FREQS - 1)[:NBINS - 1].astype(jnp.int32) + 1
        return jnp.sort(chosen)
    return jax.vmap(one_row)(keys).astype(jnp.int32)


def draw_trig_pair(key, part):
    owners = BLOCKS
    slots = owners * PCAP
    lists = BLOCKS * HALVES
    boost = jax.random.randint(jax.random.fold_in(key, 31), (owners,), 0, 4)
    forced = jax.random.randint(jax.random.fold_in(key, 32), (), 0, owners)
    slot_owner = jnp.arange(slots, dtype=jnp.int32) // PCAP
    noise = jax.random.randint(jax.random.fold_in(key, 33), (lists, slots), 0, 1024)
    score = boost[slot_owner][None, :] * 1024 + noise + jnp.where(slot_owner == forced, 8192, 0)[None, :]
    score = score * slots + jnp.arange(slots, dtype=jnp.int32)[None, :]
    unused, picked = lax.top_k(score, TRIG_DEV)
    shuffle_keys = jax.random.split(jax.random.fold_in(key, 34), lists)
    order = jax.vmap(lambda row_key: jax.random.permutation(row_key, TRIG_DEV))(shuffle_keys)
    picked = jnp.take_along_axis(picked, order, axis=1)
    within = jax.random.randint(jax.random.fold_in(key, 35), (lists, TRIG_DEV), 0, PAIR_DEV)
    result = picked // PCAP * PAIR_DEV + within
    return result.reshape(BLOCKS, HALVES, TRIG_DEV).astype(jnp.int32)


def place_ends(drawn, rng, smallest, largest):
    longest = drawn.shape.index(max(drawn.shape))
    spots = []
    for shift in (0, 1):
        where = [jax.random.randint(jax.random.fold_in(rng, axis), (), 0, length) for axis, length in enumerate(drawn.shape)]
        where[longest] = (where[longest] + shift) % drawn.shape[longest]
        spots.append(tuple(where))
    return drawn.at[spots[0]].set(smallest).at[spots[1]].set(largest)


def level_of(stream_key, shape, cuts, smallest, largest):
    loudness, own = 1.0, jax.random.fold_in(stream_key, 6)
    for axis_at, parts in cuts:
        draws = jnp.exp(jax.random.uniform(jax.random.fold_in(own, axis_at), (parts,), jnp.float32, smallest / len(cuts), largest / len(cuts)))
        loudness = loudness * jnp.repeat(draws, shape[axis_at] // parts).reshape([-1 if axis == axis_at else 1 for axis in range(len(shape))])
    return loudness


def scatter_about(stream_key, dims, spread, limit, cuts=(), kind=jnp.bfloat16):
    loudness = level_of(stream_key, dims, cuts, -0.22, 0.18) if cuts else 1.0
    entries = jax.random.normal(stream_key, dims, jnp.float32) * spread * loudness
    return jnp.minimum(jnp.maximum(entries, -limit), limit).astype(kind)


def setup_inputs(seed: int = 0, part: int = 0) -> dict:
    splits = jax.random.split(jax.random.key(seed), 7)
    own_keys = jax.random.split(jax.random.fold_in(splits[6], part), 7)
    data = scatter_about(own_keys[0], (PAIRS, FMAJ, 2 * FMIN), 1.0, 6.0, ((0, 8),))
    templates = draw_templates(jax.random.fold_in(jax.random.fold_in(splits[6], part), 71), part)
    bin_cuts = draw_bin_cuts(jax.random.fold_in(jax.random.fold_in(splits[6], part), 71), part)
    trig_template = place_ends(jax.random.randint(own_keys[3], (BLOCKS, HALVES, TRIG_DEV), 0, TEMPLATES), jax.random.fold_in(own_keys[3], 1), 0, TEMPLATES - 1).astype(jnp.int32)
    trig_pair = draw_trig_pair(jax.random.fold_in(jax.random.fold_in(splits[6], part), 71), part)
    trig_tile = place_ends(jax.random.randint(own_keys[5], (BLOCKS, HALVES, TRIG_DEV), 0, TILES), jax.random.fold_in(own_keys[5], 1), 0, TILES - 1).astype(jnp.int32)
    return {"data": data, "templates": templates, "bin_cuts": bin_cuts, "trig_template": trig_template, "trig_pair": trig_pair, "trig_tile": trig_tile}


def phase_table(rows, cols, period):
    index = jnp.arange(rows, dtype=jnp.int32)[:, None] * jnp.arange(cols, dtype=jnp.int32)[None, :] % period
    angle = index.astype(jnp.float32) * (2.0 * math.pi / period)
    return (jnp.cos(angle), jnp.sin(angle))

def second_matrix(steps, n_minor):
    index = jnp.arange(n_minor, dtype=jnp.int32)[:, None] * steps[None, :] % n_minor
    angle = index.astype(jnp.float32) * (2.0 * math.pi / n_minor)
    cosine = jnp.cos(angle)
    sine = jnp.sin(angle)
    upper = jnp.concatenate([cosine, sine], axis=1)
    lower = jnp.concatenate([-sine, cosine], axis=1)
    return jnp.concatenate([upper, lower], axis=0).astype(jnp.bfloat16)

def make_tables(n_major, n_minor):
    cos_major, sin_major = phase_table(n_major, n_major, n_major)
    twid_cos, twid_sin = phase_table(n_major, n_minor, n_major * n_minor)
    return (cos_major.astype(jnp.bfloat16), sin_major.astype(jnp.bfloat16), twid_cos, twid_sin)

def conj_product(rows, tmpl):
    n_minor = rows.shape[-1] // 2
    data_re = rows[..., :n_minor].astype(jnp.float32)
    data_im = rows[..., n_minor:].astype(jnp.float32)
    tmpl_re = tmpl[..., :n_minor].astype(jnp.float32)
    tmpl_im = tmpl[..., n_minor:].astype(jnp.float32)
    real_part = data_re * tmpl_re + data_im * tmpl_im
    imag_part = data_im * tmpl_re - data_re * tmpl_im
    return jnp.concatenate([real_part, imag_part], axis=-1).astype(jnp.bfloat16)

def first_section(spectra, tables):
    cos_major, sin_major, twid_cos, twid_sin = tables
    n_minor = spectra.shape[-1] // 2
    wide = spectra.astype(jnp.float32)
    cos_part = jnp.einsum('...ic,ia->...ac', wide, cos_major.astype(jnp.float32), precision=lax.Precision.HIGHEST)
    sin_part = jnp.einsum('...ic,ia->...ac', wide, sin_major.astype(jnp.float32), precision=lax.Precision.HIGHEST)
    real_part = cos_part[..., :n_minor] - sin_part[..., n_minor:]
    imag_part = sin_part[..., :n_minor] + cos_part[..., n_minor:]
    turned_re = real_part * twid_cos - imag_part * twid_sin
    turned_im = real_part * twid_sin + imag_part * twid_cos
    return jnp.concatenate([turned_re, turned_im], axis=-1).astype(jnp.bfloat16)

def chi_block(rows, tmpl, cuts, starts, tables, n_bins, n_steps):
    n_major = rows.shape[1]
    n_minor = rows.shape[2] // 2
    spectra = conj_product(rows, tmpl)
    freq = n_minor * jnp.arange(n_major, dtype=jnp.int32)[:, None] + jnp.arange(n_minor, dtype=jnp.int32)[None, :]
    which = lax.optimization_barrier(jnp.sum((cuts[:, :, None, None] <= freq[None, None]).astype(jnp.int32), axis=1))
    member = which[:, None] == jnp.arange(n_bins, dtype=jnp.int32)[None, :, None, None]
    member = jnp.concatenate([member, member], axis=-1)
    masked = jnp.where(member, spectra[:, None], jnp.zeros((), jnp.bfloat16))
    sectioned = first_section(masked, tables)
    steps = starts[:, None] + jnp.arange(n_steps, dtype=jnp.int32)[None, :]
    mats = jax.vmap(lambda values: second_matrix(values, n_minor))(steps)
    binned = jnp.einsum('rbac,rcs->rbas', sectioned.astype(jnp.float32), mats.astype(jnp.float32), precision=lax.Precision.HIGHEST)
    bin_re = binned[..., :n_steps]
    bin_im = binned[..., n_steps:]
    total_re = lax.optimization_barrier(jnp.sum(bin_re, axis=1))
    total_im = lax.optimization_barrier(jnp.sum(bin_im, axis=1))
    norms = lax.optimization_barrier(jnp.sum(jnp.square(tmpl.astype(jnp.float32)), axis=(1, 2)))
    diff_re = bin_re - total_re[:, None] / n_bins
    diff_im = bin_im - total_im[:, None] / n_bins
    chisq = n_bins * lax.optimization_barrier(jnp.sum(diff_re * diff_re + diff_im * diff_im, axis=1)) / norms[:, None, None]
    reduced = chisq / (2.0 * n_bins - 2.0)
    rho = jnp.sqrt(total_re * total_re + total_im * total_im) / jnp.sqrt(norms)[:, None, None]
    weighted = jnp.where(reduced > 1.0, rho * ((1.0 + reduced ** 3) * 0.5) ** (-1.0 / 6.0), rho)
    return jnp.transpose(weighted, (0, 2, 1)).reshape(rows.shape[0], -1)

def reference(data, templates, bin_cuts, trig_template, trig_pair, trig_tile):
    tables = make_tables(FMAJ, FMIN)
    second = second_matrix(jnp.arange(FMIN, dtype=jnp.int32), FMIN)
    norms = lax.optimization_barrier(jnp.sum(jnp.square(templates.astype(jnp.float32)), axis=(1, 2)))

    def scan_step(peak, index):
        spectra = conj_product(data, templates[index][None])
        sectioned = first_section(spectra, tables)
        result = jnp.einsum('pac,cs->pas', sectioned.astype(jnp.float32), second.astype(jnp.float32), precision=lax.Precision.HIGHEST)
        power = (result[..., :FMIN] ** 2 + result[..., FMIN:] ** 2) / norms[index]
        return (jnp.maximum(peak, power), None)
    peak, unused = lax.scan(scan_step, jnp.zeros((PAIRS, FMAJ, FMIN), jnp.float32), jnp.arange(TEMPLATES, dtype=jnp.int32))
    peak_snr = jnp.transpose(jnp.sqrt(peak), (0, 2, 1)).reshape(PAIRS, FREQS)
    pair_ids = trig_pair.reshape(-1, TRIG_DEV).astype(jnp.int32)
    starts = (jnp.arange(HALVES, dtype=jnp.int32)[None, :, None] * (FMIN // HALVES) + trig_tile * TILE_STEPS).reshape(-1, TRIG_DEV)
    tmpl_ids = trig_template.reshape(-1, TRIG_DEV)

    def per_list(packed):
        ids, pairs, first_steps = packed
        return chi_block(data[pairs], templates[ids], bin_cuts[ids], first_steps, tables, NBINS, TILE_STEPS)
    chi = lax.map(per_list, (tmpl_ids, pair_ids, starts))
    chi_snr = chi.reshape(BLOCKS, HALVES, TRIG_DEV, FMAJ * TILE_STEPS)
    return (peak_snr, chi_snr)
```

```python
import functools
import math

import jax
import jax.numpy as jnp
import numpy as np
from jax import lax
from jax.experimental import pallas as pl
from jax.experimental.pallas import tpu as pltpu
from jax.sharding import PartitionSpec as P

MESH = pl.DeviceIdType.MESH
NMAJ = 16
NMIN = 128
NCUT = 16
STEPS = 8
GROUP = 8


def unit_circle(index, period):
    angle = (index % period) * (2.0 * math.pi / period)
    return np.cos(angle), np.sin(angle)


def host_tables(n_sub):
    bf16 = jnp.bfloat16
    major = np.arange(NMAJ)
    minor = np.arange(NMIN)
    cos16, sin16 = unit_circle(major[:, None] * major[None, :], NMAJ)
    eye = np.eye(GROUP)
    first = np.concatenate([np.kron(eye, cos16), np.kron(eye, sin16)], axis=1).astype(bf16)
    twc, tws = unit_circle(major[:, None] * minor[None, :], NMAJ * NMIN)
    twiddle = np.concatenate([twc, tws], axis=1).astype(np.float32)
    n_half = NMIN // n_sub
    second = []
    for half in range(n_sub):
        steps = half * n_half + np.arange(n_half)
        cosine, sine = unit_circle(steps[:, None] * minor[None, :], NMIN)
        real_rows = np.concatenate([cosine, -sine], axis=1)
        imag_rows = np.concatenate([sine, cosine], axis=1)
        second.append(np.concatenate([real_rows, imag_rows], axis=0))
    second = np.stack(second).astype(bf16)
    times = np.arange(NMAJ * STEPS)
    cosine, sine = unit_circle(minor[:, None] * times[None, :], NMAJ * NMIN)
    tile_dft = np.concatenate(
        [np.concatenate([cosine, sine], axis=1), np.concatenate([-sine, cosine], axis=1)], axis=0
    ).astype(bf16)
    rowc, rows = unit_circle(major[:, None] * (times % NMAJ)[None, :], NMAJ)
    row_phase = np.tile(np.concatenate([rowc, rows], axis=1), (GROUP, 1)).astype(bf16)
    starts = np.arange(NMIN // STEPS) * STEPS
    phc, phs = unit_circle(starts[:, None] * minor[None, :], NMIN)
    tile_phase = np.concatenate([phc, phs], axis=1).astype(np.float32)[:, None, :]
    return first, twiddle, second, tile_dft, row_phase, tile_phase


def gather_kernel(n_blk, n_det, n_sub, data, tmpl, cuts, data_out, tmpl_out, cuts_out,
                  local_sem, z_send, z_recv, x_send, x_recv, s_send, s_recv,
                  tz_send, tz_recv, ts_send, ts_recv, cz_send, cz_recv):
    b = lax.axis_index("blk")
    d = lax.axis_index("det")
    c = lax.axis_index("sub")
    pairs = data.shape[0]
    kb = tmpl.shape[0]
    hp, hk = pairs // n_sub, kb // n_sub
    other = n_sub - 1 - c

    barrier = pltpu.get_barrier_semaphore()
    for dz in range(1, n_blk):
        pl.semaphore_signal(barrier, inc=1, device_id={"blk": lax.rem(b + dz, n_blk)}, device_id_type=MESH)
    for dx in range(1, n_det):
        pl.semaphore_signal(barrier, inc=1, device_id={"det": lax.rem(d + dx, n_det)}, device_id_type=MESH)
    pl.semaphore_signal(barrier, inc=1, device_id={"sub": other}, device_id_type=MESH)

    own = b * n_det + d
    locals_ = [
        pltpu.make_async_copy(data, data_out.at[own], local_sem.at[0]),
        pltpu.make_async_copy(tmpl, tmpl_out.at[b], local_sem.at[1]),
        pltpu.make_async_copy(cuts, cuts_out.at[b], local_sem.at[2]),
    ]
    for copy in locals_:
        copy.start()
    pl.semaphore_wait(barrier, n_blk + n_det - 1)

    def remote(src, dst, send, recv, where):
        copy = pltpu.make_async_remote_copy(src_ref=src, dst_ref=dst, send_sem=send, recv_sem=recv,
                                            device_id=where, device_id_type=MESH)
        copy.start()
        return copy

    half_p = pl.ds(c * hp, hp)
    half_k = pl.ds(c * hk, hk)
    z_copies, t_copies, c_copies = {}, {}, {}
    for dz in range(1, n_blk):
        where = {"blk": lax.rem(b + dz, n_blk)}
        t_copies[dz] = remote(tmpl.at[half_k], tmpl_out.at[b, half_k], tz_send.at[dz], tz_recv.at[dz], where)
        c_copies[dz] = remote(cuts, cuts_out.at[b], cz_send.at[dz], cz_recv.at[dz], where)
    for dz in range(1, n_blk):
        where = {"blk": lax.rem(b + dz, n_blk)}
        z_copies[dz] = remote(data.at[half_p], data_out.at[own, half_p], z_send.at[dz], z_recv.at[dz], where)
    x_copies, s_copies, ts_copies = {}, {}, {}
    for dx in range(1, n_det):
        x_copies[0, dx] = remote(data.at[half_p], data_out.at[own, half_p], x_send.at[0, dx], x_recv.at[0, dx],
                                 {"det": lax.rem(d + dx, n_det)})
    for dz in range(1, n_blk):
        t_copies[dz].wait_recv()
        src_b = lax.rem(b + n_blk - dz, n_blk)
        block = tmpl_out.at[src_b, half_k]
        ts_copies[dz] = remote(block, block, ts_send.at[dz], ts_recv.at[dz], {"sub": other})
    for dz in range(1, n_blk):
        z_copies[dz].wait_recv()
        src_b = lax.rem(b + n_blk - dz, n_blk)
        block = data_out.at[src_b * n_det + d, half_p]
        for dx in range(1, n_det):
            x_copies[dz, dx] = remote(block, block, x_send.at[dz, dx], x_recv.at[dz, dx],
                                      {"det": lax.rem(d + dx, n_det)})
        s_copies[dz, 0] = remote(block, block, s_send.at[dz, 0], s_recv.at[dz, 0], {"sub": other})
    for dz in range(n_blk):
        src_b = lax.rem(b + n_blk - dz, n_blk)
        for dx in range(1, n_det):
            x_copies[dz, dx].wait_recv()
            block = data_out.at[src_b * n_det + lax.rem(d + n_det - dx, n_det), half_p]
            s_copies[dz, dx] = remote(block, block, s_send.at[dz, dx], s_recv.at[dz, dx], {"sub": other})
    for copy in list(c_copies.values()) + list(ts_copies.values()) + list(s_copies.values()):
        copy.wait_recv()
    for group in (z_copies, t_copies, c_copies, x_copies, s_copies, ts_copies):
        for copy in group.values():
            copy.wait_send()
    for copy in locals_:
        copy.wait()


def gather_all(mesh_sizes, data, tmpl, cuts):
    n_blk, n_det, n_sub = mesh_sizes
    dma = pltpu.SemaphoreType.DMA
    anywhere = pl.BlockSpec(memory_space=pl.ANY)
    return pl.pallas_call(
        functools.partial(gather_kernel, n_blk, n_det, n_sub),
        out_shape=(
            jax.ShapeDtypeStruct((n_blk * n_det,) + data.shape, data.dtype),
            jax.ShapeDtypeStruct((n_blk,) + tmpl.shape, tmpl.dtype),
            jax.ShapeDtypeStruct((n_blk,) + cuts.shape, cuts.dtype),
        ),
        in_specs=[anywhere] * 3,
        out_specs=(anywhere,) * 3,
        scratch_shapes=[
            dma((3,)),
            dma((n_blk,)), dma((n_blk,)),
            dma((n_blk, n_det)), dma((n_blk, n_det)),
            dma((n_blk, n_det)), dma((n_blk, n_det)),
            dma((n_blk,)), dma((n_blk,)),
            dma((n_blk,)), dma((n_blk,)),
            dma((n_blk,)), dma((n_blk,)),
        ],
        compiler_params=pltpu.CompilerParams(collective_id=0, has_side_effects=True),
        name="gather_all",
    )(data, tmpl, cuts)


def swap_blocks(x):
    sub = lax.broadcasted_iota(jnp.int32, x.shape, 0)
    grp = lax.broadcasted_iota(jnp.int32, x.shape, 1) // NMAJ
    rows, lanes = x.shape
    for bit in (1, 2, 4):
        up = pltpu.roll(pltpu.roll(x, rows - bit, 0), NMAJ * bit, 1)
        down = pltpu.roll(pltpu.roll(x, bit, 0), lanes - NMAJ * bit, 1)
        sb, gb = (sub & bit) != 0, (grp & bit) != 0
        x = jnp.where(jnp.logical_and(jnp.logical_not(sb), gb), up,
                      jnp.where(jnp.logical_and(sb, jnp.logical_not(gb)), down, x))
    return x


def conj_product(data, tmpl):
    dr, di = data[..., :NMIN], data[..., NMIN:]
    tr, ti = tmpl[..., :NMIN], tmpl[..., NMIN:]
    return dr * tr + di * ti, di * tr - dr * ti


def compute_kernel(ids_k, ids_p, ids_t, own, data, tmpl, cuts, first, twiddle, second, tile_dft,
                   row_phase, tile_phase, peak_out, chi_out, cut_rows, cut_scr, cut_row_tab, cut_low_tab,
                   norm_tab):
    f32, bf16 = jnp.float32, jnp.bfloat16
    half = lax.axis_index("sub")
    n_tmpl = tmpl.shape[0]
    n_blk, kb, n_cut = cuts.shape
    pairs = own.shape[0]
    n_trig = chi_out.shape[0]

    cut_rows[...] = jnp.full(cut_rows.shape, NMAJ * NMIN, jnp.int32)
    for blk in range(n_blk):
        cut_rows[blk * kb:(blk + 1) * kb, 0:n_cut] = cuts[blk]
    diag = lax.broadcasted_iota(jnp.int32, (NCUT, NMIN), 0) == lax.broadcasted_iota(jnp.int32, (NCUT, NMIN), 1)
    for k in range(n_tmpl):
        line = jnp.broadcast_to(cut_rows[k:k + 1, :], (NCUT, NMIN))
        cut_scr[k * NCUT:(k + 1) * NCUT, :] = jnp.where(diag, line, 0)
    spread = jnp.ones((NMIN, NMIN), bf16)
    every = cut_scr[...]
    cut_row_tab[...] = jnp.dot((every // NMIN).astype(f32).astype(bf16), spread, preferred_element_type=f32)
    cut_low_tab[...] = jnp.dot((every % NMIN).astype(f32).astype(bf16), spread, preferred_element_type=f32)

    wide = own[...].astype(f32).reshape(pairs, NMAJ, 2 * NMIN)
    twc = jnp.broadcast_to(twiddle[:, :NMIN][None], (pairs, NMAJ, NMIN)).reshape(pairs * NMAJ, NMIN)
    tws = jnp.broadcast_to(twiddle[:, NMIN:][None], (pairs, NMAJ, NMIN)).reshape(pairs * NMAJ, NMIN)
    n_half = second.shape[1] // 2

    def one_template(k, peak):
        row = tmpl[k].astype(f32)
        norm = jnp.sum(jnp.sum(row * row, axis=0, keepdims=True), axis=1, keepdims=True)
        norm_tab[k] = jnp.broadcast_to(norm, (1, NMIN))
        real, imag = conj_product(wide, row[None])
        real = real.reshape(pairs * NMAJ, NMIN).astype(bf16)
        imag = imag.reshape(pairs * NMAJ, NMIN).astype(bf16)
        stacked = jnp.concatenate(
            [jnp.concatenate([real, imag], axis=1), jnp.concatenate([-imag, real], axis=1)], axis=0
        )
        section = jnp.dot(first[...], stacked, preferred_element_type=f32)
        sr, si = section[:, :NMIN], section[:, NMIN:]
        turned = jnp.concatenate([sr * twc - si * tws, sr * tws + si * twc], axis=1).astype(bf16)
        snr = lax.dot_general(second[half], turned, (((1,), (1,)), ((), ())), preferred_element_type=f32)
        power = snr[:n_half] * snr[:n_half] + snr[n_half:] * snr[n_half:]
        return jnp.maximum(peak, power * (1.0 / norm))

    peak = lax.fori_loop(0, n_tmpl, one_template, jnp.zeros((n_half, pairs * NMAJ), f32), unroll=4)
    swapped = swap_blocks(jnp.sqrt(peak))
    for u in range(n_half // 8):
        peak_out[:, u * 128:(u + 1) * 128] = swapped[8 * u:8 * u + 8, :]

    lane = lax.broadcasted_iota(jnp.int32, (NCUT, NMIN), 1).astype(f32)
    sub = lax.broadcasted_iota(jnp.int32, (GROUP * NCUT, NMIN), 0) % NCUT

    def one_group(q, carry):
        specs, hots, befores, lows, norms = [], [], [], [], []
        for m in range(GROUP):
            n = q * GROUP + m
            k = ids_k[0, 0, n]
            rows = data[ids_p[0, 0, n]].astype(f32)
            row = tmpl[k].astype(f32)
            real, imag = conj_product(rows, row)
            phase = tile_phase[half * (tile_phase.shape[0] // 2) + ids_t[0, 0, n]]
            pc, ps = phase[:, :NMIN], phase[:, NMIN:]
            specs.append(jnp.concatenate([real * pc - imag * ps, real * ps + imag * pc], axis=1).astype(bf16))
            at = pl.ds(pl.multiple_of(k * NCUT, NCUT), NCUT)
            cut_row = cut_row_tab[at, :]
            base = float(m * NMAJ)
            hots.append((lane == cut_row + base).astype(f32))
            befores.append(jnp.logical_and(lane >= base, lane < cut_row + base).astype(f32))
            lows.append(cut_low_tab[at, :])
            norms.append(norm_tab[k])
        z = jnp.concatenate(specs, axis=0)
        hot = jnp.concatenate(hots, axis=0)
        cut_at = jnp.concatenate(lows, axis=0)
        hot = hot.astype(bf16)
        before = jnp.concatenate(befores, axis=0).astype(bf16)
        lanes = lax.broadcasted_iota(jnp.int32, cut_at.shape, 1).astype(f32)
        keep = lanes < cut_at
        picked = jnp.dot(hot, z, preferred_element_type=f32)
        part = jnp.concatenate(
            [jnp.where(keep, picked[:, :NMIN], 0.0), jnp.where(keep, picked[:, NMIN:], 0.0)], axis=1
        ).astype(bf16)
        g = jnp.dot(part, tile_dft[...], preferred_element_type=f32)
        turn = jnp.dot(hot, row_phase[...], preferred_element_type=f32)
        f = jnp.dot(z, tile_dft[...], preferred_element_type=f32)
        own_turn = row_phase[...].astype(f32)

        def rotate(v, w):
            vr, vi, wr, wi = v[:, :NMIN], v[:, NMIN:], w[:, :NMIN], w[:, NMIN:]
            return jnp.concatenate([vr * wr - vi * wi, vr * wi + vi * wr], axis=1)

        g = rotate(g, turn)
        f = rotate(f, own_turn)
        high = f.astype(bf16)
        low = (f - high.astype(f32)).astype(bf16)
        prefix = g + jnp.dot(
            jnp.concatenate([before, before], axis=1), jnp.concatenate([high, low], axis=0),
            preferred_element_type=f32,
        )
        prev = pltpu.roll(prefix, 1, 0)
        pr, pi = prefix[:, :NMIN], prefix[:, NMIN:]
        br = pr - jnp.where(sub == 0, 0.0, prev[:, :NMIN])
        bi = pi - jnp.where(sub == 0, 0.0, prev[:, NMIN:])
        br, bi = br.reshape(GROUP, NCUT, NMIN), bi.reshape(GROUP, NCUT, NMIN)
        tr = jnp.sum(br, axis=1, keepdims=True)
        ti = jnp.sum(bi, axis=1, keepdims=True)
        dr, di = br - tr * (1.0 / NCUT), bi - ti * (1.0 / NCUT)
        spread_sq = jnp.sum(dr * dr + di * di, axis=1)
        norm = jnp.concatenate(norms, axis=0)
        reduced = spread_sq * (NCUT / (2.0 * NCUT - 2.0)) / norm
        tr, ti = tr.reshape(GROUP, NMIN), ti.reshape(GROUP, NMIN)
        rho = jnp.sqrt((tr * tr + ti * ti) / norm)
        bend = jnp.exp(jnp.log((1.0 + reduced * reduced * reduced) * 0.5) * (-1.0 / 6.0))
        chi_out[pl.ds(pl.multiple_of(q * GROUP, GROUP), GROUP), :] = jnp.where(reduced > 1.0, rho * bend, rho)
        return carry

    lax.fori_loop(0, n_trig // GROUP, one_group, 0, unroll=2)


def compute(ids_k, ids_p, ids_t, own, data, tmpl, cuts, tables):
    n_tmpl = tmpl.shape[0]
    vmem = pl.BlockSpec(memory_space=pltpu.VMEM)
    smem = pl.BlockSpec(memory_space=pltpu.SMEM)
    n_half = tables[2].shape[1] // 2
    return pl.pallas_call(
        compute_kernel,
        out_shape=(
            jax.ShapeDtypeStruct((own.shape[0], n_half * NMAJ), jnp.float32),
            jax.ShapeDtypeStruct((ids_k.shape[-1], STEPS * NMAJ), jnp.float32),
        ),
        in_specs=[smem] * 3 + [vmem] * 10,
        out_specs=(vmem, vmem),
        scratch_shapes=[
            pltpu.VMEM((n_tmpl, NMIN), jnp.int32),
            pltpu.VMEM((n_tmpl * NCUT, NMIN), jnp.int32),
            pltpu.VMEM((n_tmpl * NCUT, NMIN), jnp.float32),
            pltpu.VMEM((n_tmpl * NCUT, NMIN), jnp.float32),
            pltpu.VMEM((n_tmpl, 1, NMIN), jnp.float32),
        ],
        compiler_params=pltpu.CompilerParams(vmem_limit_bytes=48 * 1024 * 1024),
        name="filter_and_chi",
    )(ids_k, ids_p, ids_t, own, data, tmpl, cuts, *tables)


def body(sizes, data, templates, bin_cuts, trig_template, trig_pair, trig_tile):
    tables = tuple(jnp.asarray(t) for t in host_tables(sizes[2]))
    all_data, all_tmpl, all_cuts = gather_all(sizes, data, templates, bin_cuts)
    peak, chi = compute(
        trig_template, trig_pair, trig_tile, data,
        all_data.reshape((-1,) + data.shape[1:]),
        all_tmpl.reshape((-1,) + templates.shape[1:]),
        all_cuts, tables,
    )
    return peak, chi.reshape(trig_template.shape + (chi.shape[1],))


def solution(mesh):
    sizes = (mesh.shape["blk"], mesh.shape["det"], mesh.shape["sub"])
    return jax.shard_map(
        functools.partial(body, sizes),
        mesh=mesh,
        in_specs=(
            P(("groups", "blk", "det"), None, None),
            P(("groups", "blk"), None, None),
            P(("groups", "blk"), None),
            P(("groups", "blk", "det"), "sub", None),
            P(("groups", "blk", "det"), "sub", None),
            P(("groups", "blk", "det"), "sub", None),
        ),
        out_specs=(
            P(("groups", "blk", "det"), "sub"),
            P(("groups", "blk", "det"), "sub", None, None),
        ),
        check_vma=False,
    )
```

```python
import functools
import math

import jax
import jax.numpy as jnp
import numpy as np
from jax import lax
from jax.experimental import pallas as pl
from jax.experimental.pallas import tpu as pltpu
from jax.sharding import PartitionSpec as P

MESH = pl.DeviceIdType.MESH
NMAJ = 16
NMIN = 128
NCUT = 16
STEPS = 8
GROUP = 8


def unit_circle(index, period):
    angle = (index % period) * (2.0 * math.pi / period)
    return np.cos(angle), np.sin(angle)


def host_tables(n_sub):
    bf16 = jnp.bfloat16
    major = np.arange(NMAJ)
    minor = np.arange(NMIN)
    cos16, sin16 = unit_circle(major[:, None] * major[None, :], NMAJ)
    eye = np.eye(GROUP)
    first = np.concatenate([np.kron(eye, cos16), np.kron(eye, sin16)], axis=1).astype(bf16)
    twc, tws = unit_circle(major[:, None] * minor[None, :], NMAJ * NMIN)
    twiddle = np.concatenate([twc, tws], axis=1).astype(np.float32)
    n_half = NMIN // n_sub
    second = []
    for half in range(n_sub):
        steps = half * n_half + np.arange(n_half)
        cosine, sine = unit_circle(steps[:, None] * minor[None, :], NMIN)
        real_rows = np.concatenate([cosine, -sine], axis=1)
        imag_rows = np.concatenate([sine, cosine], axis=1)
        second.append(np.concatenate([real_rows, imag_rows], axis=0))
    second = np.stack(second).astype(bf16)
    times = np.arange(NMAJ * STEPS)
    cosine, sine = unit_circle(minor[:, None] * times[None, :], NMAJ * NMIN)
    tile_dft = np.concatenate(
        [np.concatenate([cosine, sine], axis=1), np.concatenate([-sine, cosine], axis=1)], axis=0
    ).astype(bf16)
    rowc, rows = unit_circle(major[:, None] * (times % NMAJ)[None, :], NMAJ)
    row_phase = np.tile(np.concatenate([rowc, rows], axis=1), (GROUP, 1)).astype(bf16)
    starts = np.arange(NMIN // STEPS) * STEPS
    phc, phs = unit_circle(starts[:, None] * minor[None, :], NMIN)
    tile_phase = np.concatenate([phc, phs], axis=1).astype(np.float32)[:, None, :]
    return first, twiddle, second, tile_dft, row_phase, tile_phase


def swap_blocks(x):
    sub = lax.broadcasted_iota(jnp.int32, x.shape, 0)
    grp = lax.broadcasted_iota(jnp.int32, x.shape, 1) // NMAJ
    rows, lanes = x.shape
    for bit in (1, 2, 4):
        up = pltpu.roll(pltpu.roll(x, rows - bit, 0), NMAJ * bit, 1)
        down = pltpu.roll(pltpu.roll(x, bit, 0), lanes - NMAJ * bit, 1)
        sb, gb = (sub & bit) != 0, (grp & bit) != 0
        x = jnp.where(jnp.logical_and(jnp.logical_not(sb), gb), up,
                      jnp.where(jnp.logical_and(sb, jnp.logical_not(gb)), down, x))
    return x


def conj_product(data, tmpl):
    dr, di = data[..., :NMIN], data[..., NMIN:]
    tr, ti = tmpl[..., :NMIN], tmpl[..., NMIN:]
    return dr * tr + di * ti, di * tr - dr * ti


def fused_kernel(n_blk, n_det, n_sub, *refs):
    (ids_k_in, ids_p_in, ids_t_in, own_in, tmpl_in, cuts_in, first_in, twiddle_in, second_in, tile_dft_in,
     row_phase_in, tile_phase_in, peak_out, chi_out, data4, tmpl4, cuts, ids_k, ids_p, ids_t, first, twiddle,
     second, tile_dft, row_phase, tile_phase, cut_rows, cut_scr, cut_row_tab, cut_low_tab, norm_tab,
     local_sem, z_send, z_recv, x_send, x_recv, s_send, s_recv, tz_send, tz_recv, ts_send, ts_recv,
     cz_send, cz_recv) = refs
    f32, bf16 = jnp.float32, jnp.bfloat16
    b = lax.axis_index("blk")
    d = lax.axis_index("det")
    half = lax.axis_index("sub")
    other = n_sub - 1 - half
    pairs = own_in.shape[0]
    kb = tmpl_in.shape[0]
    n_cut = cuts_in.shape[1]
    n_tmpl = n_blk * kb
    n_trig = chi_out.shape[0]
    hp, hk = pairs // n_sub, kb // n_sub
    own = b * n_det + d

    barrier = pltpu.get_barrier_semaphore()
    for dz in range(1, n_blk):
        pl.semaphore_signal(barrier, inc=1, device_id={"blk": lax.rem(b + dz, n_blk)}, device_id_type=MESH)
    for dx in range(1, n_det):
        pl.semaphore_signal(barrier, inc=1, device_id={"det": lax.rem(d + dx, n_det)}, device_id_type=MESH)
    pl.semaphore_signal(barrier, inc=1, device_id={"sub": other}, device_id_type=MESH)

    moves = [(tmpl_in, tmpl4.at[pl.ds(b * kb, kb)]), (own_in, data4.at[pl.ds(own * pairs, pairs)]), (cuts_in, cuts.at[b]), (first_in, first),
             (twiddle_in, twiddle), (second_in.at[half], second), (tile_dft_in, tile_dft), (row_phase_in, row_phase),
             (tile_phase_in, tile_phase), (ids_k_in, ids_k), (ids_p_in, ids_p), (ids_t_in, ids_t)]
    fetches = [pltpu.make_async_copy(src, dst, local_sem.at[i]) for i, (src, dst) in enumerate(moves)]
    for copy in fetches:
        copy.start()
    for copy in fetches[:3]:
        copy.wait()
    pl.semaphore_wait(barrier, n_blk + n_det - 1)

    def remote(ref, send, recv, where):
        copy = pltpu.make_async_remote_copy(src_ref=ref, dst_ref=ref, send_sem=send, recv_sem=recv,
                                            device_id=where, device_id_type=MESH)
        copy.start()
        return copy

    def data_half(place):
        return data4.at[pl.ds(place * pairs + half * hp, hp)]

    def tmpl_half(place):
        return tmpl4.at[pl.ds(place * kb + half * hk, hk)]

    z_copies, t_copies, c_copies, x_copies, s_copies, ts_copies = {}, {}, {}, {}, {}, {}
    for dz in range(1, n_blk):
        where = {"blk": lax.rem(b + dz, n_blk)}
        t_copies[dz] = remote(tmpl_half(b), tz_send.at[dz], tz_recv.at[dz], where)
        c_copies[dz] = remote(cuts.at[b], cz_send.at[dz], cz_recv.at[dz], where)
    for dz in range(1, n_blk):
        where = {"blk": lax.rem(b + dz, n_blk)}
        z_copies[dz] = remote(data_half(own), z_send.at[dz], z_recv.at[dz], where)
    for dx in range(1, n_det):
        x_copies[0, dx] = remote(data_half(own), x_send.at[0, dx], x_recv.at[0, dx],
                                 {"det": lax.rem(d + dx, n_det)})
    for copy in fetches[3:]:
        copy.wait()

    wide = data4[pl.ds(own * pairs, pairs)].astype(f32)
    twc = jnp.broadcast_to(twiddle[:, :NMIN][None], (pairs, NMAJ, NMIN)).reshape(pairs * NMAJ, NMIN)
    tws = jnp.broadcast_to(twiddle[:, NMIN:][None], (pairs, NMAJ, NMIN)).reshape(pairs * NMAJ, NMIN)
    n_half = second.shape[0] // 2

    def peak_of(src_b, peak):
        def one_template(k, peak):
            row = tmpl4[src_b * kb + k].astype(f32)
            norm = jnp.sum(jnp.sum(row * row, axis=0, keepdims=True), axis=1, keepdims=True)
            norm_tab[src_b * kb + k] = jnp.broadcast_to(norm, (1, NMIN))
            real, imag = conj_product(wide, row[None])
            real = real.reshape(pairs * NMAJ, NMIN).astype(bf16)
            imag = imag.reshape(pairs * NMAJ, NMIN).astype(bf16)
            stacked = jnp.concatenate(
                [jnp.concatenate([real, imag], axis=1), jnp.concatenate([-imag, real], axis=1)], axis=0
            )
            section = jnp.dot(first[...], stacked, preferred_element_type=f32)
            sr, si = section[:, :NMIN], section[:, NMIN:]
            turned = jnp.concatenate([sr * twc - si * tws, sr * tws + si * twc], axis=1).astype(bf16)
            snr = lax.dot_general(second[...], turned, (((1,), (1,)), ((), ())), preferred_element_type=f32)
            power = snr[:n_half] * snr[:n_half] + snr[n_half:] * snr[n_half:]
            return jnp.maximum(peak, power * (1.0 / norm))

        return lax.fori_loop(0, kb, one_template, peak, unroll=True)

    peak = peak_of(b, jnp.zeros((n_half, pairs * NMAJ), f32))
    for dz in range(1, n_blk):
        t_copies[dz].wait_recv()
        src_b = lax.rem(b + n_blk - dz, n_blk)
        ts_copies[dz] = remote(tmpl_half(src_b), ts_send.at[dz], ts_recv.at[dz], {"sub": other})
    for dz in range(1, n_blk):
        z_copies[dz].wait_recv()
        src_b = lax.rem(b + n_blk - dz, n_blk)
        block = data_half(src_b * n_det + d)
        for dx in range(1, n_det):
            x_copies[dz, dx] = remote(block, x_send.at[dz, dx], x_recv.at[dz, dx],
                                      {"det": lax.rem(d + dx, n_det)})
        s_copies[dz, 0] = remote(block, s_send.at[dz, 0], s_recv.at[dz, 0], {"sub": other})
        ts_copies[dz].wait_recv()
        peak = peak_of(src_b, peak)

    for copy in c_copies.values():
        copy.wait_recv()
    cut_rows[...] = jnp.full(cut_rows.shape, NMAJ * NMIN, jnp.int32)
    for blk in range(n_blk):
        cut_rows[blk * kb:(blk + 1) * kb, 0:n_cut] = cuts[blk]
    diag = lax.broadcasted_iota(jnp.int32, (NCUT, NMIN), 0) == lax.broadcasted_iota(jnp.int32, (NCUT, NMIN), 1)
    for k in range(n_tmpl):
        line = jnp.broadcast_to(cut_rows[k:k + 1, :], (NCUT, NMIN))
        cut_scr[k * NCUT:(k + 1) * NCUT, :] = jnp.where(diag, line, 0)
    spread = jnp.ones((NMIN, NMIN), bf16)
    every = cut_scr[...]
    cut_row_tab[...] = jnp.dot(
        (every >> 7).astype(f32).astype(bf16), spread, preferred_element_type=f32
    ).reshape(n_tmpl, NCUT, NMIN)
    cut_low_tab[...] = jnp.dot(
        (every & (NMIN - 1)).astype(f32).astype(bf16), spread, preferred_element_type=f32
    ).reshape(n_tmpl, NCUT, NMIN)

    for dz in range(n_blk):
        src_b = lax.rem(b + n_blk - dz, n_blk)
        for dx in range(1, n_det):
            x_copies[dz, dx].wait_recv()
            block = data_half(src_b * n_det + lax.rem(d + n_det - dx, n_det))
            s_copies[dz, dx] = remote(block, s_send.at[dz, dx], s_recv.at[dz, dx], {"sub": other})

    swapped = swap_blocks(jnp.sqrt(peak))
    for u in range(n_half // 8):
        peak_out[:, u * 128:(u + 1) * 128] = swapped[8 * u:8 * u + 8, :]
    for copy in s_copies.values():
        copy.wait_recv()

    lane = lax.broadcasted_iota(jnp.int32, (NCUT, NMIN), 1).astype(f32)
    sub = lax.broadcasted_iota(jnp.int32, (GROUP * NCUT, NMIN), 0) % NCUT

    def one_group(q, carry):
        specs, hots, befores, lows, norms = [], [], [], [], []
        for m in range(GROUP):
            n = q * GROUP + m
            k = ids_k[0, 0, n]
            rows = data4[ids_p[0, 0, n]].astype(f32)
            row = tmpl4[k].astype(f32)
            real, imag = conj_product(rows, row)
            phase = tile_phase[half * (tile_phase.shape[0] // 2) + ids_t[0, 0, n]]
            pc, ps = phase[:, :NMIN], phase[:, NMIN:]
            specs.append(jnp.concatenate([real * pc - imag * ps, real * ps + imag * pc], axis=1).astype(bf16))
            cut_row = cut_row_tab[k]
            base = float(m * NMAJ)
            hots.append((lane == cut_row + base).astype(f32))
            befores.append(jnp.logical_and(lane >= base, lane < cut_row + base).astype(f32))
            lows.append(cut_low_tab[k])
            norms.append(norm_tab[k])
        z = jnp.concatenate(specs, axis=0)
        hot = jnp.concatenate(hots, axis=0)
        cut_at = jnp.concatenate(lows, axis=0)
        hot = hot.astype(bf16)
        before = jnp.concatenate(befores, axis=0).astype(bf16)
        lanes = lax.broadcasted_iota(jnp.int32, cut_at.shape, 1).astype(f32)
        keep = lanes < cut_at
        picked = jnp.dot(hot, z, preferred_element_type=f32)
        part = jnp.concatenate(
            [jnp.where(keep, picked[:, :NMIN], 0.0), jnp.where(keep, picked[:, NMIN:], 0.0)], axis=1
        ).astype(bf16)
        g = jnp.dot(part, tile_dft[...], preferred_element_type=f32)
        turn = jnp.dot(hot, row_phase[...], preferred_element_type=f32)
        f = jnp.dot(z, tile_dft[...], preferred_element_type=f32)
        own_turn = row_phase[...].astype(f32)

        def rotate(v, w):
            vr, vi, wr, wi = v[:, :NMIN], v[:, NMIN:], w[:, :NMIN], w[:, NMIN:]
            return jnp.concatenate([vr * wr - vi * wi, vr * wi + vi * wr], axis=1)

        g = rotate(g, turn)
        f = rotate(f, own_turn)
        high = f.astype(bf16)
        low = (f - high.astype(f32)).astype(bf16)
        prefix = g + jnp.dot(
            jnp.concatenate([before, before], axis=1), jnp.concatenate([high, low], axis=0),
            preferred_element_type=f32,
        )
        prev = pltpu.roll(prefix, 1, 0)
        pr, pi = prefix[:, :NMIN], prefix[:, NMIN:]
        br = pr - jnp.where(sub == 0, 0.0, prev[:, :NMIN])
        bi = pi - jnp.where(sub == 0, 0.0, prev[:, NMIN:])
        br, bi = br.reshape(GROUP, NCUT, NMIN), bi.reshape(GROUP, NCUT, NMIN)
        tr = jnp.sum(br, axis=1, keepdims=True)
        ti = jnp.sum(bi, axis=1, keepdims=True)
        dr, di = br - tr * (1.0 / NCUT), bi - ti * (1.0 / NCUT)
        spread_sq = jnp.sum(dr * dr + di * di, axis=1)
        norm = jnp.concatenate(norms, axis=0)
        reduced = spread_sq * (NCUT / (2.0 * NCUT - 2.0)) / norm
        tr, ti = tr.reshape(GROUP, NMIN), ti.reshape(GROUP, NMIN)
        rho = jnp.sqrt((tr * tr + ti * ti) / norm)
        bend = jnp.exp(jnp.log((1.0 + reduced * reduced * reduced) * 0.5) * (-1.0 / 6.0))
        chi_out[pl.ds(pl.multiple_of(q * GROUP, GROUP), GROUP), :] = jnp.where(reduced > 1.0, rho * bend, rho)
        return carry

    lax.fori_loop(0, n_trig // GROUP, one_group, 0, unroll=2)

    for group in (z_copies, t_copies, c_copies, x_copies, s_copies, ts_copies):
        for copy in group.values():
            copy.wait_send()


def fused(sizes, ids_k, ids_p, ids_t, own, tmpl, cuts, tables):
    n_blk, n_det, n_sub = sizes
    n_tmpl = n_blk * tmpl.shape[0]
    anywhere = pl.BlockSpec(memory_space=pl.ANY)
    vmem = pl.BlockSpec(memory_space=pltpu.VMEM)
    dma = pltpu.SemaphoreType.DMA
    n_half = tables[2].shape[1] // 2
    scratch = [
        pltpu.VMEM((n_blk * n_det * own.shape[0],) + own.shape[1:], own.dtype),
        pltpu.VMEM((n_tmpl,) + tmpl.shape[1:], tmpl.dtype),
        pltpu.VMEM((n_blk,) + cuts.shape, cuts.dtype),
    ]
    scratch += [pltpu.SMEM(ids_k.shape, jnp.int32)] * 3
    for i, table in enumerate(tables):
        scratch.append(pltpu.VMEM(table.shape[1:] if i == 2 else table.shape, table.dtype))
    scratch += [
        pltpu.VMEM((n_tmpl, NMIN), jnp.int32),
        pltpu.VMEM((n_tmpl * NCUT, NMIN), jnp.int32),
        pltpu.VMEM((n_tmpl, NCUT, NMIN), jnp.float32),
        pltpu.VMEM((n_tmpl, NCUT, NMIN), jnp.float32),
        pltpu.VMEM((n_tmpl, 1, NMIN), jnp.float32),
        dma((12,)),
        dma((n_blk,)), dma((n_blk,)),
        dma((n_blk, n_det)), dma((n_blk, n_det)),
        dma((n_blk, n_det)), dma((n_blk, n_det)),
        dma((n_blk,)), dma((n_blk,)),
        dma((n_blk,)), dma((n_blk,)),
        dma((n_blk,)), dma((n_blk,)),
    ]
    return pl.pallas_call(
        functools.partial(fused_kernel, n_blk, n_det, n_sub),
        out_shape=(
            jax.ShapeDtypeStruct((own.shape[0], n_half * NMAJ), jnp.float32),
            jax.ShapeDtypeStruct((ids_k.shape[-1], STEPS * NMAJ), jnp.float32),
        ),
        in_specs=[anywhere] * 12,
        out_specs=(vmem, vmem),
        scratch_shapes=scratch,
        compiler_params=pltpu.CompilerParams(
            collective_id=0, has_side_effects=True, vmem_limit_bytes=60 * 1024 * 1024
        ),
        name="filter_and_chi",
    )(ids_k, ids_p, ids_t, own, tmpl, cuts, *tables)


def body(sizes, data, templates, bin_cuts, trig_template, trig_pair, trig_tile):
    tables = tuple(jnp.asarray(t) for t in host_tables(sizes[2]))
    peak, chi = fused(sizes, trig_template, trig_pair, trig_tile, data, templates, bin_cuts, tables)
    return peak, chi.reshape(trig_template.shape + (chi.shape[1],))


def solution(mesh):
    sizes = (mesh.shape["blk"], mesh.shape["det"], mesh.shape["sub"])
    return jax.shard_map(
        functools.partial(body, sizes),
        mesh=mesh,
        in_specs=(
            P(("groups", "blk", "det"), None, None),
            P(("groups", "blk"), None, None),
            P(("groups", "blk"), None),
            P(("groups", "blk", "det"), "sub", None),
            P(("groups", "blk", "det"), "sub", None),
            P(("groups", "blk", "det"), "sub", None),
        ),
        out_specs=(
            P(("groups", "blk", "det"), "sub"),
            P(("groups", "blk", "det"), "sub", None, None),
        ),
        check_vma=False,
    )
```

```python
import functools
import math

import jax
import jax.numpy as jnp
import numpy as np
from jax import lax
from jax.experimental import pallas as pl
from jax.experimental.pallas import tpu as pltpu
from jax.sharding import PartitionSpec as P

MESH = pl.DeviceIdType.MESH
NMAJ = 16
NMIN = 128
NCUT = 16
STEPS = 8
GROUP = 8


def unit_circle(index, period):
    angle = (index % period) * (2.0 * math.pi / period)
    return np.cos(angle), np.sin(angle)


def host_tables(n_sub):
    bf16 = jnp.bfloat16
    major = np.arange(NMAJ)
    minor = np.arange(NMIN)
    cos16, sin16 = unit_circle(major[:, None] * major[None, :], NMAJ)
    eye = np.eye(GROUP)
    first = np.concatenate([np.kron(eye, cos16), np.kron(eye, sin16)], axis=1).astype(bf16)
    twc, tws = unit_circle(major[:, None] * minor[None, :], NMAJ * NMIN)
    twiddle = np.concatenate([twc, tws], axis=1).astype(np.float32)
    n_half = NMIN // n_sub
    second = []
    for half in range(n_sub):
        steps = half * n_half + np.arange(n_half)
        cosine, sine = unit_circle(steps[:, None] * minor[None, :], NMIN)
        real_rows = np.concatenate([cosine, -sine], axis=1)
        imag_rows = np.concatenate([sine, cosine], axis=1)
        second.append(np.concatenate([real_rows, imag_rows], axis=0))
    second = np.stack(second).astype(bf16)
    times = np.arange(NMAJ * STEPS)
    cosine, sine = unit_circle(minor[:, None] * times[None, :], NMAJ * NMIN)
    tile_dft = np.concatenate(
        [np.concatenate([cosine, sine], axis=1), np.concatenate([-sine, cosine], axis=1)], axis=0
    ).astype(bf16)
    rowc, rows = unit_circle(major[:, None] * (times % NMAJ)[None, :], NMAJ)
    row_phase = np.tile(np.concatenate([rowc, rows], axis=1), (GROUP, 1)).astype(bf16)
    starts = np.arange(NMIN // STEPS) * STEPS
    phc, phs = unit_circle(starts[:, None] * minor[None, :], NMIN)
    tile_phase = np.concatenate([phc, phs], axis=1).astype(np.float32)[:, None, :]
    return first, twiddle, second, tile_dft, row_phase, tile_phase


def swap_blocks(x):
    sub = lax.broadcasted_iota(jnp.int32, x.shape, 0)
    grp = lax.broadcasted_iota(jnp.int32, x.shape, 1) // NMAJ
    rows, lanes = x.shape
    for bit in (1, 2, 4):
        up = pltpu.roll(pltpu.roll(x, rows - bit, 0), NMAJ * bit, 1)
        down = pltpu.roll(pltpu.roll(x, bit, 0), lanes - NMAJ * bit, 1)
        sb, gb = (sub & bit) != 0, (grp & bit) != 0
        x = jnp.where(jnp.logical_and(jnp.logical_not(sb), gb), up,
                      jnp.where(jnp.logical_and(sb, jnp.logical_not(gb)), down, x))
    return x


def conj_product(data, tmpl):
    dr, di = data[..., :NMIN], data[..., NMIN:]
    tr, ti = tmpl[..., :NMIN], tmpl[..., NMIN:]
    return dr * tr + di * ti, di * tr - dr * ti


def fused_kernel(n_blk, n_det, n_sub, *refs):
    (ids_k_in, ids_p_in, ids_t_in, own_in, tmpl_in, cuts_in, first_in, twiddle_in, second_in, tile_dft_in,
     row_phase_in, tile_phase_in, peak_out, chi_out, data4, tmpl4, cuts, ids_k, ids_p, ids_t, first, twiddle,
     second, tile_dft, row_phase, tile_phase, cut_rows, cut_scr, cut_row_tab, cut_low_tab, norm_tab,
     turn_tab, turned, hot_tab, before_tab, low_tab, spin_tab, scale_tab,
     local_sem, z_send, z_recv, x_send, x_recv, s_send, s_recv, tz_send, tz_recv, ts_send, ts_recv,
     cz_send, cz_recv) = refs
    f32, bf16 = jnp.float32, jnp.bfloat16
    b = lax.axis_index("blk")
    d = lax.axis_index("det")
    half = lax.axis_index("sub")
    other = n_sub - 1 - half
    pairs = own_in.shape[0]
    kb = tmpl_in.shape[0]
    n_cut = cuts_in.shape[1]
    n_tmpl = n_blk * kb
    n_trig = chi_out.shape[2]
    hp, hk = pairs // n_sub, kb // n_sub
    own = b * n_det + d

    barrier = pltpu.get_barrier_semaphore()
    for dz in range(1, n_blk):
        pl.semaphore_signal(barrier, inc=1, device_id={"blk": lax.rem(b + dz, n_blk)}, device_id_type=MESH)
    for dx in range(1, n_det):
        pl.semaphore_signal(barrier, inc=1, device_id={"det": lax.rem(d + dx, n_det)}, device_id_type=MESH)
    pl.semaphore_signal(barrier, inc=1, device_id={"sub": other}, device_id_type=MESH)

    moves = [(tmpl_in, tmpl4.at[pl.ds(b * kb, kb)]), (own_in, data4.at[pl.ds(own * pairs, pairs)]), (cuts_in, cuts.at[b]), (first_in, first),
             (twiddle_in, twiddle), (second_in.at[half], second), (tile_dft_in, tile_dft), (row_phase_in, row_phase),
             (tile_phase_in, tile_phase), (ids_k_in, ids_k), (ids_p_in, ids_p), (ids_t_in, ids_t)]
    fetches = [pltpu.make_async_copy(src, dst, local_sem.at[i]) for i, (src, dst) in enumerate(moves)]
    for copy in fetches:
        copy.start()
    for copy in fetches[:3]:
        copy.wait()
    pl.semaphore_wait(barrier, n_blk + n_det - 1)

    def remote(ref, send, recv, where):
        copy = pltpu.make_async_remote_copy(src_ref=ref, dst_ref=ref, send_sem=send, recv_sem=recv,
                                            device_id=where, device_id_type=MESH)
        copy.start()
        return copy

    def partner(step):
        index = b
        bit = 1
        while bit <= step:
            if step & bit:
                index = index + bit * (1 - 2 * lax.rem(b // bit, 2))
            bit *= 2
        return index

    def data_half(place):
        return data4.at[pl.ds(place * pairs + half * hp, hp)]

    def tmpl_half(place):
        return tmpl4.at[pl.ds(place * kb + half * hk, hk)]

    z_copies, t_copies, c_copies, x_copies, s_copies, ts_copies = {}, {}, {}, {}, {}, {}
    for dz in range(n_blk - 1, 0, -1):
        where = {"blk": partner(dz)}
        t_copies[dz] = remote(tmpl_half(b), tz_send.at[dz], tz_recv.at[dz], where)
        c_copies[dz] = remote(cuts.at[b], cz_send.at[dz], cz_recv.at[dz], where)
    for dz in range(n_blk - 1, 0, -1):
        where = {"blk": partner(dz)}
        z_copies[dz] = remote(data_half(own), z_send.at[dz], z_recv.at[dz], where)
    for dx in range(1, n_det):
        x_copies[0, dx] = remote(data_half(own), x_send.at[0, dx], x_recv.at[0, dx],
                                 {"det": lax.rem(d + dx, n_det)})
    for copy in fetches[3:]:
        copy.wait()

    wide = data4[pl.ds(own * pairs, pairs)].astype(f32)
    twc = jnp.broadcast_to(twiddle[:, :NMIN][None], (pairs, NMAJ, NMIN)).reshape(pairs * NMAJ, NMIN)
    tws = jnp.broadcast_to(twiddle[:, NMIN:][None], (pairs, NMAJ, NMIN)).reshape(pairs * NMAJ, NMIN)
    n_half = second.shape[0] // 2

    def peak_of(src_b, peak):
        def one_template(k, peak):
            row = tmpl4[src_b * kb + k].astype(f32)
            norm = jnp.sum(jnp.sum(row * row, axis=0, keepdims=True), axis=1, keepdims=True)
            norm_tab[src_b * kb + k] = jnp.broadcast_to(norm, (1, NMIN))
            real, imag = conj_product(wide, row[None])
            real = real.reshape(pairs * NMAJ, NMIN).astype(bf16)
            imag = imag.reshape(pairs * NMAJ, NMIN).astype(bf16)
            stacked = jnp.concatenate(
                [jnp.concatenate([real, imag], axis=1), jnp.concatenate([-imag, real], axis=1)], axis=0
            )
            section = jnp.dot(first[...], stacked, preferred_element_type=f32)
            sr, si = section[:, :NMIN], section[:, NMIN:]
            bent = jnp.concatenate([sr * twc - si * tws, sr * tws + si * twc], axis=1).astype(bf16)
            snr = lax.dot_general(second[...], bent, (((1,), (1,)), ((), ())), preferred_element_type=f32)
            power = snr[:n_half] * snr[:n_half] + snr[n_half:] * snr[n_half:]
            return jnp.maximum(peak, power * (1.0 / norm))

        return lax.fori_loop(0, kb, one_template, peak, unroll=True)

    peak = peak_of(b, jnp.zeros((n_half, pairs * NMAJ), f32))
    for dz in range(n_blk - 1, 0, -1):
        t_copies[dz].wait_recv()
        src_b = partner(dz)
        ts_copies[dz] = remote(tmpl_half(src_b), ts_send.at[dz], ts_recv.at[dz], {"sub": other})
    for dz in range(n_blk - 1, 0, -1):
        z_copies[dz].wait_recv()
        src_b = partner(dz)
        block = data_half(src_b * n_det + d)
        for dx in range(1, n_det):
            x_copies[dz, dx] = remote(block, x_send.at[dz, dx], x_recv.at[dz, dx],
                                      {"det": lax.rem(d + dx, n_det)})
        s_copies[dz, 0] = remote(block, s_send.at[dz, 0], s_recv.at[dz, 0], {"sub": other})
        ts_copies[dz].wait_recv()
        peak = peak_of(src_b, peak)

    for copy in c_copies.values():
        copy.wait_recv()
    cut_rows[...] = jnp.full(cut_rows.shape, NMAJ * NMIN, jnp.int32)
    for blk in range(n_blk):
        cut_rows[blk * kb:(blk + 1) * kb, 0:n_cut] = cuts[blk]
    diag = lax.broadcasted_iota(jnp.int32, (NCUT, NMIN), 0) == lax.broadcasted_iota(jnp.int32, (NCUT, NMIN), 1)
    for k in range(n_tmpl):
        line = jnp.broadcast_to(cut_rows[k:k + 1, :], (NCUT, NMIN))
        cut_scr[k * NCUT:(k + 1) * NCUT, :] = jnp.where(diag, line, 0)
    spread = jnp.ones((NMIN, NMIN), bf16)
    every = cut_scr[...]
    cut_row_tab[...] = jnp.dot(
        (every >> 7).astype(f32).astype(bf16), spread, preferred_element_type=f32
    ).reshape(n_tmpl, NCUT, NMIN)
    cut_low_tab[...] = jnp.dot(
        (every & (NMIN - 1)).astype(f32).astype(bf16), spread, preferred_element_type=f32
    ).reshape(n_tmpl, NCUT, NMIN)

    lane = lax.broadcasted_iota(jnp.int32, (NCUT, NMIN), 1).astype(f32)
    for k in range(n_tmpl * NCUT // NMIN):
        rows = slice(k * (NMIN // NCUT), (k + 1) * (NMIN // NCUT))
        row_at = cut_row_tab[rows].reshape(NMIN, NMIN)
        lanes = lax.broadcasted_iota(jnp.int32, (NMIN, NMIN), 1).astype(f32)
        turn = jnp.dot((lanes == row_at).astype(f32).astype(bf16), row_phase[...], preferred_element_type=f32)
        turn_tab[rows] = turn.reshape(NMIN // NCUT, NCUT, 2 * NMIN)

    def prepare(n, carry):
        k = ids_k[0, 0, n]
        row = tmpl4[k].astype(f32)
        phase = tile_phase[half * (tile_phase.shape[0] // n_sub) + ids_t[0, 0, n]]
        pc, ps = phase[:, :NMIN], phase[:, NMIN:]
        tr, ti = row[:, :NMIN], row[:, NMIN:]
        turned[n, :, :NMIN] = tr * pc + ti * ps
        turned[n, :, NMIN:] = tr * ps - ti * pc
        base = (lax.rem(n, GROUP) * NMAJ).astype(f32)
        cut_row = cut_row_tab[k] + base
        hot_tab[n] = (lane == cut_row).astype(f32).astype(bf16)
        before_tab[n] = jnp.logical_and(lane >= base, lane < cut_row).astype(f32).astype(bf16)
        low_tab[n] = cut_low_tab[k]
        spin_tab[n] = turn_tab[k]
        scale_tab[n] = norm_tab[k]
        return carry

    order = [0] + list(range(n_blk - 1, 0, -1))
    bounds = [n_trig * i // n_blk for i in range(n_blk + 1)]
    for turn_at, dz in enumerate(order):
        lax.fori_loop(bounds[turn_at], bounds[turn_at + 1], prepare, 0, unroll=8)
        src_b = partner(dz)
        for dx in range(1, n_det):
            x_copies[dz, dx].wait_recv()
            block = data_half(src_b * n_det + lax.rem(d + n_det - dx, n_det))
            s_copies[dz, dx] = remote(block, s_send.at[dz, dx], s_recv.at[dz, dx], {"sub": other})

    swapped = swap_blocks(jnp.sqrt(peak))
    for u in range(n_half // 8):
        peak_out[:, u * 128:(u + 1) * 128] = swapped[8 * u:8 * u + 8, :]
    for copy in s_copies.values():
        copy.wait_recv()

    sub = lax.broadcasted_iota(jnp.int32, (GROUP * NCUT, NMIN), 0) % NCUT

    def one_group(q, carry):
        group = pl.ds(q * GROUP, GROUP)
        specs = []
        for m in range(GROUP):
            n = q * GROUP + m
            rows = data4[ids_p[0, 0, n]].astype(f32)
            dr, di = rows[:, :NMIN], rows[:, NMIN:]
            wr, wi = turned[n, :, :NMIN], turned[n, :, NMIN:]
            specs.append(jnp.concatenate([dr * wr - di * wi, dr * wi + di * wr], axis=1).astype(bf16))
        z = jnp.concatenate(specs, axis=0)
        hot = hot_tab[group].reshape(GROUP * NCUT, NMIN)
        before = before_tab[group].reshape(GROUP * NCUT, NMIN)
        cut_at = low_tab[group].reshape(GROUP * NCUT, NMIN)
        turn = spin_tab[group].reshape(GROUP * NCUT, 2 * NMIN)
        lanes = lax.broadcasted_iota(jnp.int32, cut_at.shape, 1).astype(f32)
        keep = lanes < cut_at
        picked = jnp.dot(hot, z, preferred_element_type=f32)
        part = jnp.concatenate(
            [jnp.where(keep, picked[:, :NMIN], 0.0), jnp.where(keep, picked[:, NMIN:], 0.0)], axis=1
        ).astype(bf16)
        g = jnp.dot(part, tile_dft[...], preferred_element_type=f32)
        f = jnp.dot(z, tile_dft[...], preferred_element_type=f32)
        own_turn = row_phase[...].astype(f32)

        def rotate(v, w):
            vr, vi, wr, wi = v[:, :NMIN], v[:, NMIN:], w[:, :NMIN], w[:, NMIN:]
            return jnp.concatenate([vr * wr - vi * wi, vr * wi + vi * wr], axis=1)

        g = rotate(g, turn)
        f = rotate(f, own_turn)
        high = f.astype(bf16)
        low = (f - high.astype(f32)).astype(bf16)
        prefix = g + jnp.dot(
            jnp.concatenate([before, before], axis=1), jnp.concatenate([high, low], axis=0),
            preferred_element_type=f32,
        )
        prev = pltpu.roll(prefix, 1, 0)
        pr, pi = prefix[:, :NMIN], prefix[:, NMIN:]
        br = pr - jnp.where(sub == 0, 0.0, prev[:, :NMIN])
        bi = pi - jnp.where(sub == 0, 0.0, prev[:, NMIN:])
        br, bi = br.reshape(GROUP, NCUT, NMIN), bi.reshape(GROUP, NCUT, NMIN)
        tr = jnp.sum(br, axis=1, keepdims=True)
        ti = jnp.sum(bi, axis=1, keepdims=True)
        dr, di = br - tr * (1.0 / NCUT), bi - ti * (1.0 / NCUT)
        spread_sq = jnp.sum(dr * dr + di * di, axis=1)
        norm = scale_tab[group].reshape(GROUP, NMIN)
        reduced = spread_sq * (NCUT / (2.0 * NCUT - 2.0)) / norm
        tr, ti = tr.reshape(GROUP, NMIN), ti.reshape(GROUP, NMIN)
        rho = jnp.sqrt((tr * tr + ti * ti) / norm)
        bend = jnp.exp(jnp.log((1.0 + reduced * reduced * reduced) * 0.5) * (-1.0 / 6.0))
        chi_out[0, 0, pl.ds(pl.multiple_of(q * GROUP, GROUP), GROUP), :] = jnp.where(reduced > 1.0, rho * bend, rho)
        return carry

    lax.fori_loop(0, n_trig // GROUP, one_group, 0, unroll=8)

    for group in (z_copies, t_copies, c_copies, x_copies, s_copies, ts_copies):
        for copy in group.values():
            copy.wait_send()


def fused(sizes, ids_k, ids_p, ids_t, own, tmpl, cuts, tables):
    n_blk, n_det, n_sub = sizes
    n_tmpl = n_blk * tmpl.shape[0]
    n_trig = ids_k.shape[-1]
    anywhere = pl.BlockSpec(memory_space=pl.ANY)
    vmem = pl.BlockSpec(memory_space=pltpu.VMEM)
    dma = pltpu.SemaphoreType.DMA
    n_half = tables[2].shape[1] // 2
    scratch = [
        pltpu.VMEM((n_blk * n_det * own.shape[0],) + own.shape[1:], own.dtype),
        pltpu.VMEM((n_tmpl,) + tmpl.shape[1:], tmpl.dtype),
        pltpu.VMEM((n_blk,) + cuts.shape, cuts.dtype),
    ]
    scratch += [pltpu.SMEM(ids_k.shape, jnp.int32)] * 3
    for i, table in enumerate(tables):
        scratch.append(pltpu.VMEM(table.shape[1:] if i == 2 else table.shape, table.dtype))
    scratch += [
        pltpu.VMEM((n_tmpl, NMIN), jnp.int32),
        pltpu.VMEM((n_tmpl * NCUT, NMIN), jnp.int32),
        pltpu.VMEM((n_tmpl, NCUT, NMIN), jnp.float32),
        pltpu.VMEM((n_tmpl, NCUT, NMIN), jnp.float32),
        pltpu.VMEM((n_tmpl, 1, NMIN), jnp.float32),
        pltpu.VMEM((n_tmpl, NCUT, 2 * NMIN), jnp.float32),
        pltpu.VMEM((n_trig, NMAJ, 2 * NMIN), jnp.float32),
        pltpu.VMEM((n_trig, NCUT, NMIN), jnp.bfloat16),
        pltpu.VMEM((n_trig, NCUT, NMIN), jnp.bfloat16),
        pltpu.VMEM((n_trig, NCUT, NMIN), jnp.float32),
        pltpu.VMEM((n_trig, NCUT, 2 * NMIN), jnp.float32),
        pltpu.VMEM((n_trig, 1, NMIN), jnp.float32),
        dma((12,)),
        dma((n_blk,)), dma((n_blk,)),
        dma((n_blk, n_det)), dma((n_blk, n_det)),
        dma((n_blk, n_det)), dma((n_blk, n_det)),
        dma((n_blk,)), dma((n_blk,)),
        dma((n_blk,)), dma((n_blk,)),
        dma((n_blk,)), dma((n_blk,)),
    ]
    return pl.pallas_call(
        functools.partial(fused_kernel, n_blk, n_det, n_sub),
        out_shape=(
            jax.ShapeDtypeStruct((own.shape[0], n_half * NMAJ), jnp.float32),
            jax.ShapeDtypeStruct(ids_k.shape + (STEPS * NMAJ,), jnp.float32),
        ),
        in_specs=[anywhere] * 12,
        out_specs=(vmem, vmem),
        scratch_shapes=scratch,
        compiler_params=pltpu.CompilerParams(
            collective_id=0, has_side_effects=True, vmem_limit_bytes=60 * 1024 * 1024
        ),
        name="filter_and_chi",
    )(ids_k, ids_p, ids_t, own, tmpl, cuts, *tables)


def body(sizes, data, templates, bin_cuts, trig_template, trig_pair, trig_tile):
    tables = tuple(jnp.asarray(t) for t in host_tables(sizes[2]))
    peak, chi = fused(sizes, trig_template, trig_pair, trig_tile, data, templates, bin_cuts, tables)
    return peak, chi


def solution(mesh):
    sizes = (mesh.shape["blk"], mesh.shape["det"], mesh.shape["sub"])
    return jax.shard_map(
        functools.partial(body, sizes),
        mesh=mesh,
        in_specs=(
            P(("groups", "blk", "det"), None, None),
            P(("groups", "blk"), None, None),
            P(("groups", "blk"), None),
            P(("groups", "blk", "det"), "sub", None),
            P(("groups", "blk", "det"), "sub", None),
            P(("groups", "blk", "det"), "sub", None),
        ),
        out_specs=(
            P(("groups", "blk", "det"), "sub"),
            P(("groups", "blk", "det"), "sub", None, None),
        ),
        check_vma=False,
    )
```

```python
import functools
import math

import jax
import jax.numpy as jnp
import numpy as np
from jax import lax
from jax.experimental import pallas as pl
from jax.experimental.pallas import tpu as pltpu
from jax.sharding import PartitionSpec as P

MESH = pl.DeviceIdType.MESH
NMAJ = 16
NMIN = 128
NCUT = 16
STEPS = 8
GROUP = 8


def unit_circle(index, period):
    angle = (index % period) * (2.0 * math.pi / period)
    return np.cos(angle), np.sin(angle)


def host_tables(n_sub):
    bf16 = jnp.bfloat16
    major = np.arange(NMAJ)
    minor = np.arange(NMIN)
    cos16, sin16 = unit_circle(major[:, None] * major[None, :], NMAJ)
    eye = np.eye(GROUP)
    first = np.concatenate([np.kron(eye, cos16), np.kron(eye, sin16)], axis=1).astype(bf16)
    twc, tws = unit_circle(major[:, None] * minor[None, :], NMAJ * NMIN)
    twiddle = np.concatenate([twc, tws], axis=1).astype(np.float32)
    n_half = NMIN // n_sub
    second = []
    for half in range(n_sub):
        steps = half * n_half + np.arange(n_half)
        cosine, sine = unit_circle(steps[:, None] * minor[None, :], NMIN)
        real_rows = np.concatenate([cosine, -sine], axis=1)
        imag_rows = np.concatenate([sine, cosine], axis=1)
        second.append(np.concatenate([real_rows, imag_rows], axis=0))
    second = np.stack(second).astype(bf16)
    times = np.arange(NMAJ * STEPS)
    cosine, sine = unit_circle(minor[:, None] * times[None, :], NMAJ * NMIN)
    tile_dft = np.concatenate(
        [np.concatenate([cosine, sine], axis=1), np.concatenate([-sine, cosine], axis=1)], axis=0
    ).astype(bf16)
    rowc, rows = unit_circle(major[:, None] * (times % NMAJ)[None, :], NMAJ)
    row_phase = np.tile(np.concatenate([rowc, rows], axis=1), (GROUP, 1)).astype(bf16)
    starts = np.arange(NMIN // STEPS) * STEPS
    phc, phs = unit_circle(starts[:, None] * minor[None, :], NMIN)
    tile_phase = np.concatenate([phc, phs], axis=1).astype(np.float32)[:, None, :]
    return first, twiddle, second, tile_dft, row_phase, tile_phase


def swap_blocks(x):
    sub = lax.broadcasted_iota(jnp.int32, x.shape, 0)
    grp = lax.broadcasted_iota(jnp.int32, x.shape, 1) // NMAJ
    rows, lanes = x.shape
    for bit in (1, 2, 4):
        up = pltpu.roll(pltpu.roll(x, rows - bit, 0), NMAJ * bit, 1)
        down = pltpu.roll(pltpu.roll(x, bit, 0), lanes - NMAJ * bit, 1)
        sb, gb = (sub & bit) != 0, (grp & bit) != 0
        x = jnp.where(jnp.logical_and(jnp.logical_not(sb), gb), up,
                      jnp.where(jnp.logical_and(sb, jnp.logical_not(gb)), down, x))
    return x


def conj_product(data, tmpl):
    dr, di = data[..., :NMIN], data[..., NMIN:]
    tr, ti = tmpl[..., :NMIN], tmpl[..., NMIN:]
    return dr * tr + di * ti, di * tr - dr * ti


def fused_kernel(n_blk, n_det, n_sub, *refs):
    (ids_k_in, ids_p_in, ids_t_in, own_in, tmpl_in, cuts_in, first_in, twiddle_in, second_in, tile_dft_in,
     row_phase_in, tile_phase_in, peak_out, chi_out, data4, tmpl4, cuts, ids_k, ids_p, ids_t, first, twiddle,
     second, tile_dft, row_phase, tile_phase, cut_rows, cut_scr, cut_row_tab, cut_low_tab, norm_tab,
     turn_tab, turned, hot_tab, before_tab, low_tab, spin_tab, scale_tab, best,
     local_sem, z_send, z_recv, x_send, x_recv, s_send, s_recv, tz_send, tz_recv, ts_send, ts_recv,
     cz_send, cz_recv) = refs
    f32, bf16 = jnp.float32, jnp.bfloat16
    b = lax.axis_index("blk")
    d = lax.axis_index("det")
    half = lax.axis_index("sub")
    other = n_sub - 1 - half
    pairs = own_in.shape[0]
    kb = tmpl_in.shape[0]
    n_cut = cuts_in.shape[1]
    n_tmpl = n_blk * kb
    n_trig = chi_out.shape[2]
    hp, hk = pairs // n_sub, kb // n_sub
    own = b * n_det + d

    barrier = pltpu.get_barrier_semaphore()
    signs = (1, -1)

    def has(sign):
        return b < n_blk - 1 if sign == 1 else b > 0

    def beside(sign):
        return {"blk": lax.rem(b + sign + n_blk, n_blk)}

    for sign in signs:
        @pl.when(has(sign))
        def _():
            pl.semaphore_signal(barrier, inc=1, device_id=beside(sign), device_id_type=MESH)
    for dx in range(1, n_det):
        pl.semaphore_signal(barrier, inc=1, device_id={"det": lax.rem(d + dx, n_det)}, device_id_type=MESH)
    pl.semaphore_signal(barrier, inc=1, device_id={"sub": other}, device_id_type=MESH)

    moves = [(tmpl_in, tmpl4.at[pl.ds(b * kb, kb)]), (own_in, data4.at[pl.ds(own * pairs, pairs)]), (cuts_in, cuts.at[b]), (first_in, first),
             (twiddle_in, twiddle), (second_in.at[half], second), (tile_dft_in, tile_dft), (row_phase_in, row_phase),
             (tile_phase_in, tile_phase), (ids_k_in, ids_k), (ids_p_in, ids_p), (ids_t_in, ids_t)]
    fetches = [pltpu.make_async_copy(src, dst, local_sem.at[i]) for i, (src, dst) in enumerate(moves)]
    for copy in fetches:
        copy.start()
    for copy in fetches[:3]:
        copy.wait()
    pl.semaphore_wait(barrier, n_det + jnp.minimum(b, 1) + jnp.minimum(n_blk - 1 - b, 1))

    def remote(ref, send, recv, where):
        copy = pltpu.make_async_remote_copy(src_ref=ref, dst_ref=ref, send_sem=send, recv_sem=recv,
                                            device_id=where, device_id_type=MESH)
        copy.start()
        return copy

    def partner(step):
        index = b
        bit = 1
        while bit <= step:
            if step & bit:
                index = index + bit * (1 - 2 * lax.rem(b // bit, 2))
            bit *= 2
        return index

    def data_half(place):
        return data4.at[pl.ds(place * pairs + half * hp, hp)]

    def tmpl_half(place):
        return tmpl4.at[pl.ds(place * kb + half * hk, hk)]

    def ref_of(kind, place):
        if kind == 0:
            return tmpl_half(place)
        return cuts.at[place] if kind == 1 else data_half(place * n_det + d)

    sends = (tz_send, cz_send, z_send)
    recvs = (tz_recv, cz_recv, z_recv)

    def hop(kind, sign, k):
        side = signs.index(sign)
        ref = ref_of(kind, b - sign * k)
        return pltpu.make_async_remote_copy(
            src_ref=ref, dst_ref=ref, send_sem=sends[kind].at[side, k], recv_sem=recvs[kind].at[side, k],
            device_id=beside(sign), device_id_type=MESH)

    def landed(kind, sign, k):
        side = signs.index(sign)
        ref = ref_of(kind, b - sign * k)
        return pltpu.make_async_remote_copy(
            src_ref=ref, dst_ref=ref, send_sem=sends[kind].at[side, k - 1], recv_sem=recvs[kind].at[side, k - 1],
            device_id=beside(sign), device_id_type=MESH)

    def holds(sign, k):
        return b >= k if sign == 1 else b < n_blk - k

    def x_hop(place, dx):
        ref = data_half(place * n_det + d)
        return pltpu.make_async_remote_copy(
            src_ref=ref, dst_ref=ref, send_sem=x_send.at[place, dx], recv_sem=x_recv.at[place, dx],
            device_id={"det": lax.rem(d + dx, n_det)}, device_id_type=MESH)

    def s_hop(place, dx):
        ref = data_half(place * n_det + lax.rem(d + n_det - dx, n_det))
        return pltpu.make_async_remote_copy(
            src_ref=ref, dst_ref=ref, send_sem=s_send.at[place, dx], recv_sem=s_recv.at[place, dx],
            device_id={"sub": other}, device_id_type=MESH)

    def ts_hop(place):
        ref = tmpl_half(place)
        return pltpu.make_async_remote_copy(
            src_ref=ref, dst_ref=ref, send_sem=ts_send.at[place], recv_sem=ts_recv.at[place],
            device_id={"sub": other}, device_id_type=MESH)

    for kind in range(3):
        for sign in signs:
            @pl.when(has(sign))
            def _():
                hop(kind, sign, 0).start()
    for dx in range(1, n_det):
        x_hop(b, dx).start()
    for copy in fetches[3:]:
        copy.wait()

    wide = data4[pl.ds(own * pairs, pairs)].astype(f32)
    twc = jnp.broadcast_to(twiddle[:, :NMIN][None], (pairs, NMAJ, NMIN)).reshape(pairs * NMAJ, NMIN)
    tws = jnp.broadcast_to(twiddle[:, NMIN:][None], (pairs, NMAJ, NMIN)).reshape(pairs * NMAJ, NMIN)
    n_half = second.shape[0] // 2

    def peak_of(src_b, peak):
        def one_template(k, peak):
            row = tmpl4[src_b * kb + k].astype(f32)
            norm = jnp.sum(jnp.sum(row * row, axis=0, keepdims=True), axis=1, keepdims=True)
            norm_tab[src_b * kb + k] = jnp.broadcast_to(norm, (1, NMIN))
            real, imag = conj_product(wide, row[None])
            real = real.reshape(pairs * NMAJ, NMIN).astype(bf16)
            imag = imag.reshape(pairs * NMAJ, NMIN).astype(bf16)
            stacked = jnp.concatenate(
                [jnp.concatenate([real, imag], axis=1), jnp.concatenate([-imag, real], axis=1)], axis=0
            )
            section = jnp.dot(first[...], stacked, preferred_element_type=f32)
            sr, si = section[:, :NMIN], section[:, NMIN:]
            bent = jnp.concatenate([sr * twc - si * tws, sr * tws + si * twc], axis=1).astype(bf16)
            snr = lax.dot_general(second[...], bent, (((1,), (1,)), ((), ())), preferred_element_type=f32)
            power = snr[:n_half] * snr[:n_half] + snr[n_half:] * snr[n_half:]
            return jnp.maximum(peak, power * (1.0 / norm))

        return lax.fori_loop(0, kb, one_template, peak, unroll=n_blk <= 4)

    best[...] = peak_of(b, jnp.zeros((n_half, pairs * NMAJ), f32))

    def peak_behind(k):
        for sign in signs:
            @pl.when(holds(sign, k))
            def _():
                place = b - sign * k
                ts_hop(place).wait_recv()
                best[...] = peak_of(place, best[...])

    for k in range(1, n_blk):
        for kind in range(3):
            for sign in signs:
                @pl.when(holds(sign, k))
                def _():
                    place = b - sign * k
                    landed(kind, sign, k).wait_recv()

                    @pl.when(has(sign))
                    def _():
                        hop(kind, sign, k).start()

                    if kind == 0:
                        ts_hop(place).start()
                    if kind == 2:
                        for dx in range(1, n_det):
                            x_hop(place, dx).start()
                        s_hop(place, 0).start()
        if k > 1:
            peak_behind(k - 1)
    peak_behind(n_blk - 1)

    cut_rows[...] = jnp.full(cut_rows.shape, NMAJ * NMIN, jnp.int32)
    for blk in range(n_blk):
        cut_rows[blk * kb:(blk + 1) * kb, 0:n_cut] = cuts[blk]
    diag = lax.broadcasted_iota(jnp.int32, (NCUT, NMIN), 0) == lax.broadcasted_iota(jnp.int32, (NCUT, NMIN), 1)
    for k in range(n_tmpl):
        line = jnp.broadcast_to(cut_rows[k:k + 1, :], (NCUT, NMIN))
        cut_scr[k * NCUT:(k + 1) * NCUT, :] = jnp.where(diag, line, 0)
    spread = jnp.ones((NMIN, NMIN), bf16)
    every = cut_scr[...]
    cut_row_tab[...] = jnp.dot(
        (every >> 7).astype(f32).astype(bf16), spread, preferred_element_type=f32
    ).reshape(n_tmpl, NCUT, NMIN)
    cut_low_tab[...] = jnp.dot(
        (every & (NMIN - 1)).astype(f32).astype(bf16), spread, preferred_element_type=f32
    ).reshape(n_tmpl, NCUT, NMIN)

    lane = lax.broadcasted_iota(jnp.int32, (NCUT, NMIN), 1).astype(f32)
    for k in range(n_tmpl * NCUT // NMIN):
        rows = slice(k * (NMIN // NCUT), (k + 1) * (NMIN // NCUT))
        row_at = cut_row_tab[rows].reshape(NMIN, NMIN)
        lanes = lax.broadcasted_iota(jnp.int32, (NMIN, NMIN), 1).astype(f32)
        turn = jnp.dot((lanes == row_at).astype(f32).astype(bf16), row_phase[...], preferred_element_type=f32)
        turn_tab[rows] = turn.reshape(NMIN // NCUT, NCUT, 2 * NMIN)

    def prepare(n, carry):
        k = ids_k[0, 0, n]
        row = tmpl4[k].astype(f32)
        phase = tile_phase[half * (tile_phase.shape[0] // n_sub) + ids_t[0, 0, n]]
        pc, ps = phase[:, :NMIN], phase[:, NMIN:]
        tr, ti = row[:, :NMIN], row[:, NMIN:]
        turned[n, :, :NMIN] = tr * pc + ti * ps
        turned[n, :, NMIN:] = tr * ps - ti * pc
        base = (lax.rem(n, GROUP) * NMAJ).astype(f32)
        cut_row = cut_row_tab[k] + base
        hot_tab[n] = (lane == cut_row).astype(f32).astype(bf16)
        before_tab[n] = jnp.logical_and(lane >= base, lane < cut_row).astype(f32).astype(bf16)
        low_tab[n] = cut_low_tab[k]
        spin_tab[n] = turn_tab[k]
        scale_tab[n] = norm_tab[k]
        return carry

    order = range(n_blk)
    bounds = [n_trig * i // n_blk for i in range(n_blk + 1)]
    for turn_at, dz in enumerate(order):
        lax.fori_loop(bounds[turn_at], bounds[turn_at + 1], prepare, 0, unroll=8)
        src_b = partner(dz)
        for dx in range(1, n_det):
            x_hop(src_b, dx).wait_recv()
            s_hop(src_b, dx).start()

    swapped = swap_blocks(jnp.sqrt(best[...]))
    peak_out[...] = swapped
    for place in range(n_blk):
        for dx in range(n_det):
            if dx > 0:
                s_hop(place, dx).wait_recv()
            else:
                @pl.when(b != place)
                def _():
                    s_hop(place, 0).wait_recv()

    sub = lax.broadcasted_iota(jnp.int32, (GROUP * NCUT, NMIN), 0) % NCUT

    def one_group(q, carry):
        group = pl.ds(q * GROUP, GROUP)
        specs = []
        for m in range(GROUP):
            n = q * GROUP + m
            rows = data4[ids_p[0, 0, n]].astype(f32)
            dr, di = rows[:, :NMIN], rows[:, NMIN:]
            wr, wi = turned[n, :, :NMIN], turned[n, :, NMIN:]
            specs.append(jnp.concatenate([dr * wr - di * wi, dr * wi + di * wr], axis=1).astype(bf16))
        z = jnp.concatenate(specs, axis=0)
        hot = hot_tab[group].reshape(GROUP * NCUT, NMIN)
        before = before_tab[group].reshape(GROUP * NCUT, NMIN)
        cut_at = low_tab[group].reshape(GROUP * NCUT, NMIN)
        turn = spin_tab[group].reshape(GROUP * NCUT, 2 * NMIN)
        lanes = lax.broadcasted_iota(jnp.int32, cut_at.shape, 1).astype(f32)
        keep = lanes < cut_at
        picked = jnp.dot(hot, z, preferred_element_type=f32)
        part = jnp.concatenate(
            [jnp.where(keep, picked[:, :NMIN], 0.0), jnp.where(keep, picked[:, NMIN:], 0.0)], axis=1
        ).astype(bf16)
        g = jnp.dot(part, tile_dft[...], preferred_element_type=f32)
        f = jnp.dot(z, tile_dft[...], preferred_element_type=f32)
        own_turn = row_phase[...].astype(f32)

        def rotate(v, w):
            vr, vi, wr, wi = v[:, :NMIN], v[:, NMIN:], w[:, :NMIN], w[:, NMIN:]
            return jnp.concatenate([vr * wr - vi * wi, vr * wi + vi * wr], axis=1)

        g = rotate(g, turn)
        f = rotate(f, own_turn)
        high = f.astype(bf16)
        low = (f - high.astype(f32)).astype(bf16)
        prefix = g + jnp.dot(
            jnp.concatenate([before, before], axis=1), jnp.concatenate([high, low], axis=0),
            preferred_element_type=f32,
        )
        prev = pltpu.roll(prefix, 1, 0)
        pr, pi = prefix[:, :NMIN], prefix[:, NMIN:]
        br = pr - jnp.where(sub == 0, 0.0, prev[:, :NMIN])
        bi = pi - jnp.where(sub == 0, 0.0, prev[:, NMIN:])
        br, bi = br.reshape(GROUP, NCUT, NMIN), bi.reshape(GROUP, NCUT, NMIN)
        tr = jnp.sum(br, axis=1, keepdims=True)
        ti = jnp.sum(bi, axis=1, keepdims=True)
        dr, di = br - tr * (1.0 / NCUT), bi - ti * (1.0 / NCUT)
        spread_sq = jnp.sum(dr * dr + di * di, axis=1)
        norm = scale_tab[group].reshape(GROUP, NMIN)
        reduced = spread_sq * (NCUT / (2.0 * NCUT - 2.0)) / norm
        tr, ti = tr.reshape(GROUP, NMIN), ti.reshape(GROUP, NMIN)
        rho = jnp.sqrt((tr * tr + ti * ti) / norm)
        bend = jnp.exp(jnp.log((1.0 + reduced * reduced * reduced) * 0.5) * (-1.0 / 6.0))
        chi_out[0, 0, pl.ds(pl.multiple_of(q * GROUP, GROUP), GROUP), :] = jnp.where(reduced > 1.0, rho * bend, rho)
        return carry

    lax.fori_loop(0, n_trig // GROUP, one_group, 0, unroll=8)

    for k in range(n_blk):
        for sign in signs:
            @pl.when(jnp.logical_and(holds(sign, k), has(sign)))
            def _():
                for kind in range(3):
                    hop(kind, sign, k).wait_send()
    for place in range(n_blk):
        for dx in range(1, n_det):
            x_hop(place, dx).wait_send()
            s_hop(place, dx).wait_send()

        @pl.when(b != place)
        def _():
            s_hop(place, 0).wait_send()
            ts_hop(place).wait_send()


def fused(sizes, ids_k, ids_p, ids_t, own, tmpl, cuts, tables):
    n_blk, n_det, n_sub = sizes
    n_tmpl = n_blk * tmpl.shape[0]
    n_trig = ids_k.shape[-1]
    anywhere = pl.BlockSpec(memory_space=pl.ANY)
    vmem = pl.BlockSpec(memory_space=pltpu.VMEM)
    dma = pltpu.SemaphoreType.DMA
    n_half = tables[2].shape[1] // 2
    scratch = [
        pltpu.VMEM((n_blk * n_det * own.shape[0],) + own.shape[1:], own.dtype),
        pltpu.VMEM((n_tmpl,) + tmpl.shape[1:], tmpl.dtype),
        pltpu.VMEM((n_blk,) + cuts.shape, cuts.dtype),
    ]
    scratch += [pltpu.SMEM(ids_k.shape, jnp.int32)] * 3
    for i, table in enumerate(tables):
        scratch.append(pltpu.VMEM(table.shape[1:] if i == 2 else table.shape, table.dtype))
    scratch += [
        pltpu.VMEM((n_tmpl, NMIN), jnp.int32),
        pltpu.VMEM((n_tmpl * NCUT, NMIN), jnp.int32),
        pltpu.VMEM((n_tmpl, NCUT, NMIN), jnp.float32),
        pltpu.VMEM((n_tmpl, NCUT, NMIN), jnp.float32),
        pltpu.VMEM((n_tmpl, 1, NMIN), jnp.float32),
        pltpu.VMEM((n_tmpl, NCUT, 2 * NMIN), jnp.float32),
        pltpu.VMEM((n_trig, NMAJ, 2 * NMIN), jnp.float32),
        pltpu.VMEM((n_trig, NCUT, NMIN), jnp.bfloat16),
        pltpu.VMEM((n_trig, NCUT, NMIN), jnp.bfloat16),
        pltpu.VMEM((n_trig, NCUT, NMIN), jnp.float32),
        pltpu.VMEM((n_trig, NCUT, 2 * NMIN), jnp.float32),
        pltpu.VMEM((n_trig, 1, NMIN), jnp.float32),
        pltpu.VMEM((n_half, own.shape[0] * NMAJ), jnp.float32),
        dma((12,)),
        dma((2, n_blk)), dma((2, n_blk)),
        dma((n_blk, n_det)), dma((n_blk, n_det)),
        dma((n_blk, n_det)), dma((n_blk, n_det)),
        dma((2, n_blk)), dma((2, n_blk)),
        dma((n_blk,)), dma((n_blk,)),
        dma((2, n_blk)), dma((2, n_blk)),
    ]
    return pl.pallas_call(
        functools.partial(fused_kernel, n_blk, n_det, n_sub),
        out_shape=(
            jax.ShapeDtypeStruct((n_half, own.shape[0] * NMAJ), jnp.float32),
            jax.ShapeDtypeStruct(ids_k.shape + (STEPS * NMAJ,), jnp.float32),
        ),
        in_specs=[anywhere] * 12,
        out_specs=(vmem, vmem),
        scratch_shapes=scratch,
        compiler_params=pltpu.CompilerParams(
            collective_id=0, has_side_effects=True, vmem_limit_bytes=60 * 1024 * 1024
        ),
        name="filter_and_chi",
    )(ids_k, ids_p, ids_t, own, tmpl, cuts, *tables)


def body(sizes, data, templates, bin_cuts, trig_template, trig_pair, trig_tile):
    tables = tuple(jnp.asarray(t) for t in host_tables(sizes[2]))
    peak, chi = fused(sizes, trig_template, trig_pair, trig_tile, data, templates, bin_cuts, tables)
    pairs = data.shape[0]
    peak = peak.reshape(-1, pairs, peak.shape[1]).transpose(1, 0, 2).reshape(pairs, -1)
    return peak, chi


def solution(mesh):
    sizes = (mesh.shape["blk"], mesh.shape["det"], mesh.shape["sub"])
    return jax.shard_map(
        functools.partial(body, sizes),
        mesh=mesh,
        in_specs=(
            P(("groups", "blk", "det"), None, None),
            P(("groups", "blk"), None, None),
            P(("groups", "blk"), None),
            P(("groups", "blk", "det"), "sub", None),
            P(("groups", "blk", "det"), "sub", None),
            P(("groups", "blk", "det"), "sub", None),
        ),
        out_specs=(
            P(("groups", "blk", "det"), "sub"),
            P(("groups", "blk", "det"), "sub", None, None),
        ),
        check_vma=False,
    )
```
